256 devices in a mesh: side: 2 (over x_lo), grp: 8 (over z), blk: 16 (over y, x_hi, core).
Axes of the slice: x: 4 (x_hi: 2, x_lo: 2; x = x_hi * 2 + x_lo), y: 4, z: 8, core: 2. Of those that a mesh axis runs over, the one named last changes fastest.
Arguments:
- embed_codes: bfloat16 [2, 65536, 128], P('side', ('grp', 'blk')), may hold values from -4 to 4
- embed_exps: int32 [2, 512], P('side', ('grp', 'blk')), may hold values from -1 to 1
- degrees: int32 [2, 65536], P('side', ('grp', 'blk')), may hold values from 16 to 128
- adjacency: bfloat16 [2, 49152, 128, 128], P('side', ('grp', 'blk')), may hold values from 0 to 1
- block_index: int32 [2, 2, 49152], P('side', None, ('grp', 'blk')), may hold values from 0 to 64, as said below
Outputs:
- layer_rows: bfloat16 [2, 65536, 128], P('side', ('grp', 'blk'))
The draws below stay inside these ranges and needn't reach their ends.
Inputs may be any that keep to these rules, and one draw needn't show every extreme that they name: `block_index`: each device's list of 384 slots: its used slots come first, in non-decreasing source tile (row 1 below 64), with distinct (destination, source) pairs and destination tiles below 32; the remaining slots have source 64 and destination 0. Every list uses 384 // 4 slots or more, and in each section one list uses all 384.
All inputs are finite; a program needn't handle non-finite values.
Results may differ from the reference program's by a relative error of at most 0.0048.
Values may be sent and summed in bfloat16 or wider, within the bound.
A program may use at most 128 MiB of HBM per device.

```python
import jax
import jax.numpy as jnp
from jax import lax

W = 128
TILE = 128
TPS = 4
DEVS = 128
NODES = 65536
SRC_TILES = 64
DST_TILES = 32
MAXB = 384
N_GRP = 8
N_BLK = 16


def device_list(key, filled):
    key_heat, key_score, key_used = jax.random.split(key, 3)
    pair_count = DST_TILES * SRC_TILES
    pairs = jnp.arange(pair_count, dtype=jnp.int32)
    source_tile = pairs % SRC_TILES
    target_tile = pairs // SRC_TILES
    heat = jax.random.randint(key_heat, (SRC_TILES // TPS,), 0, 4)
    score = jax.random.randint(key_score, (pair_count,), 0, 1024) + heat[source_tile // TPS] * 1024
    score = score * pair_count + pairs
    used_count = jnp.where(filled, MAXB, MAXB - jax.random.randint(key_used, (), 0, MAXB - MAXB // 4 + 1))
    _, order = lax.top_k(score, MAXB)
    ranks = jnp.arange(MAXB, dtype=jnp.int32)
    keeping = ranks < used_count
    chosen_source = jnp.where(keeping, source_tile[order], SRC_TILES)
    chosen_target = jnp.where(keeping, target_tile[order], 0)
    arrange = jnp.argsort(chosen_source * MAXB + ranks, stable=True)
    return jnp.stack([chosen_target[arrange], chosen_source[arrange]])


def draw_block_index(key, part):
    full_device = jax.random.randint(jax.random.fold_in(key, 11), (2,), 0, DEVS)
    device_keys = jax.random.split(jax.random.fold_in(key, 12), 2 * DEVS)
    marks = (jnp.arange(DEVS)[None, :] == full_device[:, None]).reshape(2 * DEVS)
    lists = jax.vmap(device_list)(device_keys, marks)
    lists = lists.reshape(2, DEVS, 2, MAXB).transpose(0, 2, 1, 3)
    return lists.reshape(2, 2, DEVS * MAXB).astype(jnp.int32)


def touch_ends(entries, stream_key, low, largest):
    dims = entries.shape
    index_at = [jax.random.randint(jax.random.fold_in(stream_key, axis), (), 0, dims[axis]) for axis in range(len(dims))]
    entries = entries.at[tuple(index_at)].set(low)
    longest = dims.index(max(dims))
    index_at[longest] = (index_at[longest] + 1) % dims[longest]
    return entries.at[tuple(index_at)].set(largest)


def shard_levels(key, shape, cuts, smallest, largest):
    def one(axis_at, shards_of):
        steps = jax.random.uniform(jax.random.fold_in(jax.random.fold_in(key, 6), axis_at), (shards_of,), jnp.float32, smallest / len(cuts), largest / len(cuts))
        return jnp.repeat(jnp.exp(steps), shape[axis_at] // shards_of).reshape((-1,) + (1,) * (len(shape) - axis_at - 1))

    level = one(*cuts[0])
    for cut in cuts[1:]:
        level = level * one(*cut)
    return level


def noise(stream_key, shape, deviation, bound, shards=(), held_as=jnp.bfloat16):
    drawn = deviation * jax.random.normal(stream_key, shape, jnp.float32)
    if shards:
        drawn = drawn * shard_levels(stream_key, shape, shards, -0.22, 0.18)
    return jnp.clip(drawn, -bound, bound).astype(held_as)


def setup_inputs(seed: int = 0) -> dict:
    keys = jax.random.split(jax.random.key(seed), 6)
    return {
        "embed_codes": noise(keys[0], (2, NODES, W), 1.0, 4.0, ((0, 2), (1, 128))),
        "embed_exps": touch_ends(jax.random.randint(keys[1], (2, NODES // TILE), -1, 2), jax.random.fold_in(keys[1], 1), -1, 1).astype(jnp.int32),
        "degrees": touch_ends(jax.random.randint(keys[2], (2, NODES), 16, 129), jax.random.fold_in(keys[2], 1), 16, 128).astype(jnp.int32),
        "adjacency": jnp.clip(1.0 * jax.random.uniform(keys[3], (2, DEVS * MAXB, TILE, TILE), jnp.float32) ** shard_levels(keys[3], (2, DEVS * MAXB, TILE, TILE), ((0, 2), (1, 128)), -0.2, 0.2), 0.0, 1.0).astype(jnp.bfloat16),
        "block_index": draw_block_index(jax.random.fold_in(keys[5], 71), 0),
    }


def reference(embed_codes, embed_exps, degrees, adjacency, block_index):
    tile_rows = adjacency.shape[2]
    row_width = embed_codes.shape[2]
    scale = jnp.repeat(jnp.exp2(embed_exps.astype(jnp.float32)), tile_rows, axis=1)
    inverse = lax.rsqrt(degrees.astype(jnp.float32))
    source_rows = (embed_codes.astype(jnp.float32) * scale[..., None] * inverse[..., None]).astype(jnp.bfloat16)
    results = []
    for section in range(2):
        source = source_rows[1 - section].reshape(N_GRP, SRC_TILES, tile_rows, row_width)
        grid = adjacency[section].reshape(N_GRP, N_BLK, MAXB, tile_rows, tile_rows)
        listed = block_index[section].reshape(2, N_GRP, N_BLK, MAXB)

        def one_group(running, group):
            tiles, group_blocks, targets, sources = group

            def one_device(device):
                dev_blocks, dev_targets, dev_sources = device
                active = dev_sources < SRC_TILES
                picked = tiles[jnp.minimum(dev_sources, SRC_TILES - 1)].astype(jnp.float32)
                products = jnp.einsum('kij,kjw->kiw', dev_blocks.astype(jnp.float32), picked)
                products = jnp.where(active[:, None, None], products, jnp.zeros_like(products))
                return jax.ops.segment_sum(products, dev_targets, num_segments=DST_TILES)
            partial_sums = lax.map(one_device, (group_blocks, targets, sources))
            return (running + partial_sums, None)
        starting = jnp.zeros((N_BLK, DST_TILES, tile_rows, row_width), jnp.float32)
        running, _ = lax.scan(one_group, starting, (source, grid, listed[0], listed[1]))
        running = running.reshape(N_BLK, N_GRP, TPS * tile_rows, row_width)
        running = running.transpose(1, 0, 2, 3).reshape(NODES, row_width)
        results.append((running * inverse[section][:, None]).astype(jnp.bfloat16))
    return jnp.stack(results)
```

```python
import functools

import jax
import jax.numpy as jnp
from jax import lax
from jax.experimental import pallas as pl
from jax.experimental.pallas import tpu as pltpu
from jax.sharding import PartitionSpec as P

MESH = pl.DeviceIdType.MESH
TILE = 128
TPS = 4
ROWS = TILE * TPS
HALF = ROWS // 2
QUARTER = HALF // 2
NY, NH, NC = 4, 2, 2
GROUPS = 8
DST = 32
SLOTS = 384
ADJ_PIECES = 8
DGROUP = 8


def kernel(
    codes_ref, exps_ref, deg_ref, adj_ref, index_ref, out_ref,
    a_ref, s_ref, t_ref, own_ref, acc_ref, inv_ref, tblv_ref, tbl_ref,
    ring_out, ring_in,
    adj_sem, tbl_sem,
    xa_s, xa_r, xb_s, xb_r, ya_s, ya_r, yr_s, yr_r, t_s, t_r, tr_s, tr_r,
    sib_s, sib_r, ring_s, ring_r,
):
    side = lax.axis_index("side")
    grp = lax.axis_index("grp")
    blk = lax.axis_index("blk")
    y, h, c = blk // (NH * NC), (blk // NC) % NH, blk % NC
    other = 1 - side

    def at(yy, hh, cc):
        return (yy * NH + hh) * NC + cc

    yu, yd, yo = (y + 1) % NY, (y + NY - 1) % NY, (y + 2) % NY
    gu, gd = (grp + 1) % GROUPS, (grp + GROUPS - 1) % GROUPS
    hs = (h, 1 - h)
    to_x = [(other, grp, at(y, hh, c)) for hh in hs]
    to_y = [(side, grp, at(yu, h, c)), (side, grp, at(yd, h, c))]
    to_sib = (side, grp, at(y, h, 1 - c))
    to_z = [(side, gu, blk), (side, gd, blk)]

    adj_copies = []
    per = SLOTS // ADJ_PIECES
    for piece in range(ADJ_PIECES):
        cut = pl.ds(piece * per, per)
        copy = pltpu.make_async_copy(adj_ref.at[cut], a_ref.at[cut], adj_sem.at[piece])
        copy.start()
        adj_copies.append(copy)

    barrier = pltpu.get_barrier_semaphore()
    partners = [*to_x, *to_y, to_sib, *to_z]
    for target in partners:
        pl.semaphore_signal(barrier, inc=1, device_id=target, device_id_type=MESH)

    for tile in range(TPS):
        lanes = deg_ref[0:1, tile * TILE:(tile + 1) * TILE].astype(jnp.float32)
        inverse = jnp.transpose(jnp.broadcast_to(lax.rsqrt(lanes), (TILE, TILE)))
        inv_ref[pl.ds(tile * TILE, TILE), :] = inverse
        power = jnp.exp2(jnp.full((TILE, TILE), exps_ref[0, tile], jnp.int32).astype(jnp.float32))
        rows = codes_ref[0, pl.ds(tile * TILE, TILE), :].astype(jnp.float32)
        rows = (rows * power * inverse).astype(jnp.bfloat16)
        if tile < TPS // 2:
            own_ref[pl.ds(tile * TILE, TILE), :] = rows
        else:
            t_ref[y, pl.ds((tile - TPS // 2) * TILE, TILE), :] = rows

    pl.semaphore_wait(barrier, len(partners))

    sends = []

    def send(src, dst, ssem, rsem, target):
        copy = pltpu.make_async_remote_copy(
            src_ref=src, dst_ref=dst, send_sem=ssem, recv_sem=rsem,
            device_id=target, device_id_type=MESH,
        )
        copy.start()
        sends.append(copy)

    def wait_in(dst, rsem):
        pltpu.make_async_copy(dst, dst, rsem).wait()

    def a_rows(yy, hh, cc):
        return s_ref.at[at(yy, hh, cc), pl.ds(0, HALF)]

    def b_rows(yy, hh, cc):
        return s_ref.at[at(yy, hh, cc), pl.ds(HALF, HALF)]

    for i in range(2):
        send(own_ref, a_rows(y, h, c), xa_s.at[i], xa_r.at[i], to_x[i])
        send(t_ref.at[y], t_ref.at[y], t_s.at[i], t_r.at[i], to_y[i])
    for i in range(2):
        send(t_ref.at[y], b_rows(y, h, c), xb_s.at[0, i], xb_r.at[0, i], to_x[i])

    flat = (
        lax.broadcasted_iota(jnp.int32, (NY * NH * NC, TILE), 0) * TILE
        + lax.broadcasted_iota(jnp.int32, (NY * NH * NC, TILE), 1)
    )

    def note(step, table):
        for j in range(16):
            k = step * 16 + j
            place = index_ref[0, 1, k] * DST + index_ref[0, 0, k]
            table = jnp.where(flat == place, k, table)
        return table

    tblv_ref[...] = lax.fori_loop(0, SLOTS // 16, note, jnp.full(flat.shape, SLOTS, jnp.int32))
    tbl_copy = pltpu.make_async_copy(tblv_ref, tbl_ref, tbl_sem)
    tbl_copy.start()
    a_ref[SLOTS] = jnp.zeros((TILE, TILE), jnp.bfloat16)
    acc_ref[...] = jnp.zeros_like(acc_ref)

    def product(source):
        rows = s_ref[source]

        def some(step, carry):
            parts = []
            for j in range(DGROUP):
                d = step * DGROUP + j
                parts.append(jnp.concatenate(
                    [a_ref[tbl_ref[source, q * DST + d]] for q in range(TPS)], axis=1))
            left = jnp.concatenate(parts, axis=0)
            cut = pl.ds(step * (DGROUP * TILE), DGROUP * TILE)
            acc_ref[cut, :] += jnp.dot(left, rows, preferred_element_type=jnp.float32)
            return carry

        lax.fori_loop(0, DST // DGROUP, some, 0)

    ys = (y, yu, yd, yo)

    def hand(number, ref):
        send(ref, ref, sib_s.at[number], sib_r.at[number], to_sib)

    def sib_in(number):
        k = number % 8
        rows = a_rows if number < 8 else b_rows
        wait_in(rows(ys[k // 2], hs[k % 2], 1 - c), sib_r.at[number])

    for i in range(2):
        frm = yd if i == 0 else yu
        wait_in(t_ref.at[frm], t_r.at[i])
        quarter = t_ref.at[frm, pl.ds(i * QUARTER, QUARTER)]
        send(quarter, quarter, tr_s.at[i], tr_r.at[i], to_y[i])
    for i in range(2):
        ref = a_rows(y, hs[i], c)
        wait_in(ref, xa_r.at[i])
        for v in range(2):
            send(ref, ref, ya_s.at[v, i], ya_r.at[v, i], to_y[v])
        hand(i, ref)
    for n, frm in ((1, yu), (2, yd)):
        for i in range(2):
            send(t_ref.at[frm], b_rows(frm, h, c), xb_s.at[n, i], xb_r.at[n, i], to_x[i])
    tbl_copy.wait()
    for copy in adj_copies:
        copy.wait()
    for i in range(2):
        ref = b_rows(y, hs[i], c)
        wait_in(ref, xb_r.at[0, i])
        hand(8 + i, ref)
    for i in range(2):
        product(at(y, hs[i], c))
    for i in range(2):
        wait_in(t_ref.at[yo, pl.ds(i * QUARTER, QUARTER)], tr_r.at[i])
    for i in range(2):
        send(t_ref.at[yo], b_rows(yo, h, c), xb_s.at[3, i], xb_r.at[3, i], to_x[i])
    for i in range(2):
        sib_in(i)
        sib_in(8 + i)
        product(at(y, hs[i], 1 - c))
    for i in range(2):
        for v in range(2):
            frm = yd if v == 0 else yu
            ref = a_rows(frm, hs[i], c)
            wait_in(ref, ya_r.at[v, i])
            if i == v:
                send(ref, ref, yr_s.at[i], yr_r.at[i], to_y[v])
            hand((4 if v == 0 else 2) + i, ref)
    for n, frm in ((1, yu), (2, yd)):
        for i in range(2):
            ref = b_rows(frm, hs[i], c)
            wait_in(ref, xb_r.at[n, i])
            hand(8 + 2 * n + i, ref)
    for n, frm in ((1, yu), (2, yd)):
        for i in range(2):
            product(at(frm, hs[i], c))
    for i in range(2):
        ref = b_rows(yo, hs[i], c)
        wait_in(ref, xb_r.at[3, i])
        hand(14 + i, ref)
    for n, frm in ((1, yu), (2, yd)):
        for i in range(2):
            sib_in(2 * n + i)
            sib_in(8 + 2 * n + i)
            product(at(frm, hs[i], 1 - c))
    for i in range(2):
        ref = a_rows(yo, hs[i], c)
        wait_in(ref, yr_r.at[i])
        hand(6 + i, ref)
    for i in range(2):
        product(at(yo, hs[i], c))
    for i in range(2):
        sib_in(6 + i)
        sib_in(14 + i)
        product(at(yo, hs[i], 1 - c))

    for m in range(7):
        reach = 4 - (m + 1) // 2
        for way in range(2):
            part = (m % 2) ^ way
            dest = (grp + reach) % GROUPS if way == 0 else (grp + GROUPS - reach) % GROUPS
            value = acc_ref[pl.ds(dest * ROWS + part * HALF, HALF), :]
            if m >= 2:
                wait_in(ring_in.at[way, m - 2], ring_r.at[way, m - 2])
                value = value + ring_in[way, m - 2].astype(jnp.float32)
            ring_out[way, m] = value.astype(jnp.bfloat16)
            send(ring_out.at[way, m], ring_in.at[way, m], ring_s.at[way, m], ring_r.at[way, m], to_z[way])
    for way in range(2):
        wait_in(ring_in.at[way, 5], ring_r.at[way, 5])
    for way in range(2):
        wait_in(ring_in.at[way, 6], ring_r.at[way, 6])
    for part in range(2):
        value = acc_ref[pl.ds(grp * ROWS + part * HALF, HALF), :]
        value = value + ring_in[part, 6].astype(jnp.float32)
        value = value + ring_in[1 - part, 5].astype(jnp.float32)
        value = value * inv_ref[pl.ds(part * HALF, HALF), :]
        out_ref[0, pl.ds(part * HALF, HALF), :] = value.astype(jnp.bfloat16)
    for copy in sends:
        copy.wait_send()


def shards(embed_codes, embed_exps, degrees, adjacency, block_index):
    width = embed_codes.shape[2]
    dma = pltpu.SemaphoreType.DMA
    vmem = pl.BlockSpec(memory_space=pltpu.VMEM)
    smem = pl.BlockSpec(memory_space=pltpu.SMEM)
    return pl.pallas_call(
        kernel,
        out_shape=jax.ShapeDtypeStruct(embed_codes.shape, jnp.bfloat16),
        in_specs=[vmem, smem, vmem, pl.BlockSpec(memory_space=pl.ANY), smem],
        out_specs=vmem,
        scratch_shapes=[
            pltpu.VMEM((SLOTS + 1, TILE, TILE), jnp.bfloat16),
            pltpu.VMEM((NY * NH * NC, ROWS, width), jnp.bfloat16),
            pltpu.VMEM((NY, HALF, width), jnp.bfloat16),
            pltpu.VMEM((HALF, width), jnp.bfloat16),
            pltpu.VMEM((DST * TILE, width), jnp.float32),
            pltpu.VMEM((ROWS, width), jnp.float32),
            pltpu.VMEM((NY * NH * NC, TILE), jnp.int32),
            pltpu.SMEM((NY * NH * NC, TILE), jnp.int32),
            pltpu.VMEM((2, 7, HALF, width), jnp.bfloat16),
            pltpu.VMEM((2, 7, HALF, width), jnp.bfloat16),
            dma((ADJ_PIECES,)), dma(()),
            dma((2,)), dma((2,)), dma((4, 2)), dma((4, 2)), dma((2, 2)), dma((2, 2)),
            dma((2,)), dma((2,)), dma((2,)), dma((2,)), dma((2,)), dma((2,)),
            dma((16,)), dma((16,)), dma((2, 7)), dma((2, 7)),
        ],
        compiler_params=pltpu.CompilerParams(
            collective_id=0, has_side_effects=True, vmem_limit_bytes=48 * 2**20
        ),
    )(embed_codes, embed_exps, degrees, adjacency.reshape(adjacency.shape[1:]), block_index)


def solution(mesh):
    placed = (
        P("side", ("grp", "blk"), None),
        P("side", ("grp", "blk")),
        P("side", ("grp", "blk")),
        P("side", ("grp", "blk"), None, None),
        P("side", None, ("grp", "blk")),
    )
    return jax.shard_map(
        shards,
        mesh=mesh,
        in_specs=placed,
        out_specs=P("side", ("grp", "blk"), None),
        check_vma=False,
    )
```

```python
import functools

import jax
import jax.numpy as jnp
from jax import lax
from jax.experimental import pallas as pl
from jax.experimental.pallas import tpu as pltpu
from jax.sharding import PartitionSpec as P

MESH = pl.DeviceIdType.MESH
TILE = 128
TPS = 4
ROWS = TILE * TPS
HALF = ROWS // 2
NY, NH, NC = 4, 2, 2
GROUPS = 8
DST = 32
SLOTS = 384
ADJ_PIECES = 8
PAIRS = (SLOTS + DST) // 2
UNROLL = 8
NSRC = 64


def kernel(
    codes_hbm, exps_hbm, deg_hbm, adj_ref, index_hbm, out_ref,
    a_ref, s_ref, t_ref, own_ref, sum_ref, inv_ref, tblv_ref, tbl_ref,
    codes_ref, exps_ref, deg_ref, index_ref,
    ring_out, ring_in,
    in_sem, adj_sem, tbl_sem,
    xa_s, xa_r, xb_s, xb_r, ya_s, ya_r, yr_s, yr_r, t_s, t_r, tr_s, tr_r,
    sib_s, sib_r, ring_s, ring_r,
):
    side = lax.axis_index("side")
    grp = lax.axis_index("grp")
    blk = lax.axis_index("blk")
    y, h, c = blk // (NH * NC), (blk // NC) % NH, blk % NC
    other = 1 - side

    def at(yy, hh, cc):
        return (yy * NH + hh) * NC + cc

    yu, yd, yo = (y + 1) % NY, (y + NY - 1) % NY, (y + 2) % NY
    gu, gd = (grp + 1) % GROUPS, (grp + GROUPS - 1) % GROUPS
    hs = (h, 1 - h)
    to_x = [(other, grp, at(y, hh, c)) for hh in hs]
    to_y = [(side, grp, at(yu, h, c)), (side, grp, at(yd, h, c))]
    to_sib = (side, grp, at(y, h, 1 - c))
    to_z = [(side, gu, blk), (side, gd, blk)]

    barrier = pltpu.get_barrier_semaphore()
    partners = [*to_x, *to_y, to_sib, *to_z]
    for target in partners:
        pl.semaphore_signal(barrier, inc=1, device_id=target, device_id_type=MESH)

    small = [
        pltpu.make_async_copy(src, dst, in_sem.at[i])
        for i, (src, dst) in enumerate((
            (exps_hbm, exps_ref), (deg_hbm, deg_ref), (codes_hbm, codes_ref), (index_hbm, index_ref)))
    ]
    for copy in small:
        copy.start()
    adj_copies = []
    per = SLOTS // ADJ_PIECES
    for piece in range(ADJ_PIECES):
        cut = pl.ds(piece * per, per)
        copy = pltpu.make_async_copy(adj_ref.at[cut], a_ref.at[cut], adj_sem.at[piece])
        copy.start()
        adj_copies.append(copy)

    def column(row):
        return jnp.transpose(jnp.broadcast_to(row, (TILE, TILE)))

    for copy in small[:3]:
        copy.wait()
    for tile in range(TPS):
        lanes = deg_ref[0:1, tile * TILE:(tile + 1) * TILE].astype(jnp.float32)
        inverse = column(lax.rsqrt(lanes))
        inv_ref[pl.ds(tile * TILE, TILE), :] = inverse
        power = jnp.exp2(jnp.full((TILE, TILE), exps_ref[0, tile], jnp.int32).astype(jnp.float32))
        rows = codes_ref[0, pl.ds(tile * TILE, TILE), :].astype(jnp.float32)
        rows = (rows * power * inverse).astype(jnp.bfloat16)
        if tile < TPS // 2:
            own_ref[tile] = rows
        else:
            t_ref[y, tile - TPS // 2] = rows

    pl.semaphore_wait(barrier, len(partners))

    sends = []

    def send(src, dst, ssem, rsem, target):
        copy = pltpu.make_async_remote_copy(
            src_ref=src, dst_ref=dst, send_sem=ssem, recv_sem=rsem,
            device_id=target, device_id_type=MESH,
        )
        copy.start()
        sends.append(copy)

    def wait_in(dst, rsem):
        pltpu.make_async_copy(dst, dst, rsem).wait()

    def a_rows(yy, hh, cc):
        return s_ref.at[pl.ds(at(yy, hh, cc) * TPS, TPS // 2)]

    def b_rows(yy, hh, cc):
        return s_ref.at[pl.ds(at(yy, hh, cc) * TPS + TPS // 2, TPS // 2)]

    for i in range(2):
        send(own_ref, a_rows(y, h, c), xa_s.at[i], xa_r.at[i], to_x[i])
        send(t_ref.at[y], t_ref.at[y], t_s.at[i], t_r.at[i], to_y[i])
    for i in range(2):
        send(t_ref.at[y], b_rows(y, h, c), xb_s.at[0, i], xb_r.at[0, i], to_x[i])

    small[3].wait()
    sub = lax.broadcasted_iota(jnp.int32, (TILE, TILE), 0)
    lane = lax.broadcasted_iota(jnp.int32, (TILE, TILE), 1)
    lane_row = lax.broadcasted_iota(jnp.int32, (1, TILE), 1)
    cuts = range(SLOTS // TILE)

    def down(mask, value=1):
        return jnp.sum(jnp.where(mask, value, 0), axis=0, keepdims=True)

    target = [index_ref[0, 0:1, j * TILE:(j + 1) * TILE] for j in cuts]
    source = [index_ref[0, 1:2, j * TILE:(j + 1) * TILE] for j in cuts]
    used = [q < NSRC for q in source]
    key = [jnp.where(u, t, DST) for u, t in zip(used, target)]
    key_col = [column(t) for t in key]
    count = sum(down(k == lane) for k in key_col)
    padded = jnp.where(lane_row < DST, (count + 1) // 2 * 2, 0)
    padded_col = column(padded)
    begin = down(sub < lane, padded_col)
    begin_col = column(begin)
    place_col, code_col = [], []
    for j in cuts:
        rank = down((key_col[j] == key[j]) & (sub < lane))
        for i in range(j):
            rank = rank + down(key_col[i] == key[j])
        place = down(sub < key[j], padded_col) + rank
        place_col.append(column(jnp.where(used[j], place, 8 * TILE)))
        code_col.append(((j * TILE + sub) * NSRC + column(source[j])) * 2)
    for r in range(4):
        spot = lane + r * TILE
        code = jnp.full((TILE, TILE), -1, jnp.int32)
        for j in cuts:
            code = jnp.where(place_col[j] == spot, code_col[j], code)
        code = jnp.max(code, axis=0, keepdims=True)
        first = down((begin_col == spot) & (padded_col > 0))
        tblv_ref[r:r + 1, :] = jnp.where(code < 0, SLOTS * NSRC * 2, code) + first
    tblv_ref[4:5, :] = jnp.where(padded > 0, (begin + padded) // 2 - 1, PAIRS)
    tbl_copy = pltpu.make_async_copy(tblv_ref, tbl_ref, tbl_sem)
    tbl_copy.start()
    a_ref[SLOTS] = jnp.zeros((TILE, TILE), jnp.bfloat16)
    sum_ref[PAIRS] = jnp.zeros((TILE, TILE), jnp.float32)

    def products():
        def some(step, total):
            for j in range(UNROLL):
                pair = step * UNROLL + j
                row, spot = pair // (TILE // 2), pair % (TILE // 2) * 2
                one, two = tbl_ref[row, spot], tbl_ref[row, spot + 1]
                left = jnp.concatenate([a_ref[one // (2 * NSRC)], a_ref[two // (2 * NSRC)]], axis=1)
                right = jnp.concatenate(
                    [s_ref[one // 2 % NSRC], s_ref[two // 2 % NSRC]], axis=0)
                value = jnp.dot(left, right, preferred_element_type=jnp.float32)
                keep = (1 - one % 2).astype(jnp.float32)
                total = value + total * keep
                sum_ref[pair] = total
            return total

        lax.fori_loop(0, PAIRS // UNROLL, some, jnp.zeros((TILE, TILE), jnp.float32))

    def summed(group, part):
        at_tile = group * TPS + part * (TPS // 2)
        return jnp.concatenate(
            [sum_ref[tbl_ref[4, at_tile + j]] for j in range(TPS // 2)], axis=0)

    ys = (y, yu, yd, yo)

    def hand(number, ref):
        send(ref, ref, sib_s.at[number], sib_r.at[number], to_sib)

    def sib_in(number):
        k = number % 8
        rows = a_rows if number < 8 else b_rows
        wait_in(rows(ys[k // 2], hs[k % 2], 1 - c), sib_r.at[number])

    for i in range(2):
        frm = yd if i == 0 else yu
        wait_in(t_ref.at[frm], t_r.at[i])
        tile = t_ref.at[frm, i]
        send(tile, tile, tr_s.at[i], tr_r.at[i], to_y[i])
        for v in range(2):
            send(t_ref.at[frm], b_rows(frm, h, c), xb_s.at[2 - i, v], xb_r.at[2 - i, v], to_x[v])
    for i in range(2):
        ref = a_rows(y, hs[i], c)
        wait_in(ref, xa_r.at[i])
        for v in range(2):
            send(ref, ref, ya_s.at[v, i], ya_r.at[v, i], to_y[v])
        hand(i, ref)
    for i in range(2):
        ref = b_rows(y, hs[i], c)
        wait_in(ref, xb_r.at[0, i])
        hand(8 + i, ref)
    for i in range(2):
        wait_in(t_ref.at[yo, i], tr_r.at[i])
    for i in range(2):
        send(t_ref.at[yo], b_rows(yo, h, c), xb_s.at[3, i], xb_r.at[3, i], to_x[i])
    for i in range(2):
        for v in (i, 1 - i):
            frm = yd if v == 0 else yu
            ref = a_rows(frm, hs[i], c)
            wait_in(ref, ya_r.at[v, i])
            if i == v:
                send(ref, ref, yr_s.at[i], yr_r.at[i], to_y[v])
            hand((4 if v == 0 else 2) + i, ref)
    for n, frm in ((2, yd), (1, yu)):
        for i in range(2):
            ref = b_rows(frm, hs[i], c)
            wait_in(ref, xb_r.at[n, i])
            hand(8 + 2 * n + i, ref)
    for i in range(2):
        ref = b_rows(yo, hs[i], c)
        wait_in(ref, xb_r.at[3, i])
        hand(14 + i, ref)
    for i in range(2):
        ref = a_rows(yo, hs[i], c)
        wait_in(ref, yr_r.at[i])
        hand(6 + i, ref)
    tbl_copy.wait()
    for copy in adj_copies:
        copy.wait()
    for number in range(16):
        sib_in(number)
    products()

    for m in range(7):
        reach = 4 - (m + 1) // 2
        for way in range(2):
            part = (m % 2) ^ way
            dest = (grp + reach) % GROUPS if way == 0 else (grp + GROUPS - reach) % GROUPS
            value = summed(dest, part)
            if m >= 2:
                wait_in(ring_in.at[way, m - 2], ring_r.at[way, m - 2])
                value = value + ring_in[way, m - 2].astype(jnp.float32)
            ring_out[way, m] = value.astype(jnp.bfloat16)
            send(ring_out.at[way, m], ring_in.at[way, m], ring_s.at[way, m], ring_r.at[way, m], to_z[way])
    for way in range(2):
        wait_in(ring_in.at[way, 5], ring_r.at[way, 5])
    for way in range(2):
        wait_in(ring_in.at[way, 6], ring_r.at[way, 6])
    for part in range(2):
        value = summed(grp, part)
        value = value + ring_in[part, 6].astype(jnp.float32)
        value = value + ring_in[1 - part, 5].astype(jnp.float32)
        value = value * inv_ref[pl.ds(part * HALF, HALF), :]
        out_ref[0, pl.ds(part * HALF, HALF), :] = value.astype(jnp.bfloat16)
    for copy in sends:
        copy.wait_send()


def shards(embed_codes, embed_exps, degrees, adjacency, block_index):
    width = embed_codes.shape[2]
    dma = pltpu.SemaphoreType.DMA
    vmem = pl.BlockSpec(memory_space=pltpu.VMEM)
    return pl.pallas_call(
        kernel,
        out_shape=jax.ShapeDtypeStruct(embed_codes.shape, jnp.bfloat16),
        in_specs=[pl.BlockSpec(memory_space=pltpu.HBM)] * 5,
        out_specs=vmem,
        scratch_shapes=[
            pltpu.VMEM((SLOTS + 1, TILE, TILE), jnp.bfloat16),
            pltpu.VMEM((NSRC, TILE, width), jnp.bfloat16),
            pltpu.VMEM((NY, TPS // 2, TILE, width), jnp.bfloat16),
            pltpu.VMEM((TPS // 2, TILE, width), jnp.bfloat16),
            pltpu.VMEM((PAIRS + 1, TILE, width), jnp.float32),
            pltpu.VMEM((ROWS, width), jnp.float32),
            pltpu.VMEM((8, TILE), jnp.int32),
            pltpu.SMEM((8, TILE), jnp.int32),
            pltpu.VMEM(embed_codes.shape, embed_codes.dtype),
            pltpu.SMEM(embed_exps.shape, embed_exps.dtype),
            pltpu.VMEM(degrees.shape, degrees.dtype),
            pltpu.VMEM(block_index.shape, block_index.dtype),
            pltpu.VMEM((2, 7, HALF, width), jnp.bfloat16),
            pltpu.VMEM((2, 7, HALF, width), jnp.bfloat16),
            dma((4,)), dma((ADJ_PIECES,)), dma(()),
            dma((2,)), dma((2,)), dma((4, 2)), dma((4, 2)), dma((2, 2)), dma((2, 2)),
            dma((2,)), dma((2,)), dma((2,)), dma((2,)), dma((2,)), dma((2,)),
            dma((16,)), dma((16,)), dma((2, 7)), dma((2, 7)),
        ],
        compiler_params=pltpu.CompilerParams(
            collective_id=0, has_side_effects=True, vmem_limit_bytes=67_043_328
        ),
    )(embed_codes, embed_exps, degrees, adjacency.reshape(adjacency.shape[1:]), block_index)


def solution(mesh):
    placed = (
        P("side", ("grp", "blk"), None),
        P("side", ("grp", "blk")),
        P("side", ("grp", "blk")),
        P("side", ("grp", "blk"), None, None),
        P("side", None, ("grp", "blk")),
    )
    return jax.shard_map(
        shards,
        mesh=mesh,
        in_specs=placed,
        out_specs=P("side", ("grp", "blk"), None),
        check_vma=False,
    )
```

```python
import jax
import jax.numpy as jnp
from jax import lax
from jax.experimental import pallas as pl
from jax.experimental.pallas import tpu as pltpu
from jax.sharding import PartitionSpec as P

MESH = pl.DeviceIdType.MESH
TILE = 128
TPS = 4
PART = TPS // 2
FEATS = TILE // 2
NY, NH, NC = 4, 2, 2
GROUPS = 8
DST = 32
SLOTS = 384
NSRC = 64
ADJ_PIECES = 8
PAIRS = (SLOTS + DST) // 2
SEGMENTS = ((0, 64, 32), (64, 64, 32), (128, 80, 40))


def kernel(
    codes_hbm, exps_hbm, deg_hbm, adj_ref, index_hbm, out_ref,
    a_ref, s0_ref, s1_ref, t_ref, own_ref, sum_ref, fin_ref, tblv_ref, tbl_ref,
    codes_ref, exps_ref, deg_ref, index_ref,
    ring_out, ring_in,
    in_sem, adj_sem, tbl_sem,
    xa_s, xa_r, xb_s, xb_r, ya_s, ya_r, yr_s, yr_r, t_s, t_r, tr_s, tr_r,
    sib_s, sib_r, ring_s, ring_r,
):
    s_refs = (s0_ref, s1_ref)
    side = lax.axis_index("side")
    grp = lax.axis_index("grp")
    blk = lax.axis_index("blk")
    y, h, c = blk // (NH * NC), (blk // NC) % NH, blk % NC
    other = 1 - side

    def at(yy, hh, cc):
        return (yy * NH + hh) * NC + cc

    yu, yd, yo = (y + 1) % NY, (y + NY - 1) % NY, (y + 2) % NY
    gu, gd = (grp + 1) % GROUPS, (grp + GROUPS - 1) % GROUPS
    hs = (h, 1 - h)
    to_x = [(other, grp, at(y, hh, c)) for hh in hs]
    to_y = [(side, grp, at(yu, h, c)), (side, grp, at(yd, h, c))]
    to_sib = (side, grp, at(y, h, 1 - c))
    to_z = [(side, gu, blk), (side, gd, blk)]

    barrier = pltpu.get_barrier_semaphore()
    partners = [*to_x, *to_y, to_sib, *to_z]
    for target in partners:
        pl.semaphore_signal(barrier, inc=1, device_id=target, device_id_type=MESH)

    small = [
        pltpu.make_async_copy(src, dst, in_sem.at[i])
        for i, (src, dst) in enumerate((
            (exps_hbm, exps_ref), (deg_hbm, deg_ref), (codes_hbm, codes_ref), (index_hbm, index_ref)))
    ]
    for copy in small:
        copy.start()
    adj_copies = []
    per = SLOTS // ADJ_PIECES
    for piece in range(ADJ_PIECES):
        cut = pl.ds(piece * per, per)
        copy = pltpu.make_async_copy(adj_ref.at[cut], a_ref.at[cut], adj_sem.at[piece])
        copy.start()
        adj_copies.append(copy)

    def inverse(tile):
        lanes = deg_ref[0:1, tile * TILE:(tile + 1) * TILE].astype(jnp.float32)
        return jnp.broadcast_to(lax.rsqrt(lanes), (TILE, TILE))

    for copy in small[:3]:
        copy.wait()
    for tile in range(TPS):
        power = jnp.exp2(jnp.full((TILE, TILE), exps_ref[0, tile], jnp.int32).astype(jnp.float32))
        rows = jnp.transpose(codes_ref[0, pl.ds(tile * TILE, TILE), :].astype(jnp.float32))
        rows = (rows * power * inverse(tile)).astype(jnp.bfloat16)
        for half in range(2):
            cut = rows[half * FEATS:(half + 1) * FEATS]
            if tile < PART:
                own_ref[half, tile] = cut
            else:
                t_ref[half, y, tile - PART] = cut

    pl.semaphore_wait(barrier, len(partners))

    sends = []

    def send(src, dst, ssem, rsem, target):
        copy = pltpu.make_async_remote_copy(
            src_ref=src, dst_ref=dst, send_sem=ssem, recv_sem=rsem,
            device_id=target, device_id_type=MESH,
        )
        copy.start()
        sends.append(copy)

    def wait_in(dst, rsem):
        pltpu.make_async_copy(dst, dst, rsem).wait()

    def a_rows(half, yy, hh, cc):
        return s_refs[half].at[pl.ds(at(yy, hh, cc) * TPS, PART)]

    def b_rows(half, yy, hh, cc):
        return s_refs[half].at[pl.ds(at(yy, hh, cc) * TPS + PART, PART)]

    for half in range(2):
        for i in range(2):
            send(own_ref.at[half], a_rows(half, y, h, c), xa_s.at[half, i], xa_r.at[half, i], to_x[i])
            send(t_ref.at[half, y], t_ref.at[half, y], t_s.at[half, i], t_r.at[half, i], to_y[i])
        for i in range(2):
            send(t_ref.at[half, y], b_rows(half, y, h, c), xb_s.at[half, 0, i], xb_r.at[half, 0, i], to_x[i])

    small[3].wait()
    sub = lax.broadcasted_iota(jnp.int32, (TILE, TILE), 0)
    lane = lax.broadcasted_iota(jnp.int32, (TILE, TILE), 1)
    lane_row = lax.broadcasted_iota(jnp.int32, (1, TILE), 1)
    cuts = range(SLOTS // TILE)

    def column(row):
        return jnp.transpose(jnp.broadcast_to(row, (TILE, TILE)))

    def down(mask, value=1):
        return jnp.sum(jnp.where(mask, value, 0), axis=0, keepdims=True)

    target = [index_ref[0, 0:1, j * TILE:(j + 1) * TILE] for j in cuts]
    source = [index_ref[0, 1:2, j * TILE:(j + 1) * TILE] for j in cuts]
    used = [q < NSRC for q in source]
    shift = (GROUPS + GROUPS // 2 - grp) * TPS
    key = [jnp.where(u, (t + shift) & (DST - 1), DST) for u, t in zip(used, target)]
    key_col = [column(t) for t in key]
    count = sum(down(k == lane) for k in key_col)
    padded = jnp.where(lane_row < DST, (count + 1) & ~1, 0)
    padded_col = column(padded)
    begin = down(sub < lane, padded_col)
    begin_col = column(begin)
    place_col, code_col = [], []
    for j in cuts:
        rank = down((key_col[j] == key[j]) & (sub < lane))
        for i in range(j):
            rank = rank + down(key_col[i] == key[j])
        place = down(sub < key[j], padded_col) + rank
        place_col.append(column(jnp.where(used[j], place, 8 * TILE)))
        code_col.append(((j * TILE + sub) * NSRC + column(source[j])) * 2)
    for r in range(4):
        spot = lane + r * TILE
        code = jnp.full((TILE, TILE), -1, jnp.int32)
        for j in cuts:
            code = jnp.where(place_col[j] == spot, code_col[j], code)
        code = jnp.max(code, axis=0, keepdims=True)
        first = down((begin_col == spot) & (padded_col > 0))
        tblv_ref[r:r + 1, :] = jnp.where(code < 0, SLOTS * NSRC * 2, code) + first
    tblv_ref[4:5, :] = jnp.where(padded > 0, ((begin + padded) >> 1) - 1, PAIRS)
    tbl_copy = pltpu.make_async_copy(tblv_ref, tbl_ref, tbl_sem)
    tbl_copy.start()
    a_ref[SLOTS] = jnp.zeros((TILE, TILE), jnp.bfloat16)
    for half in range(2):
        sum_ref[half, PAIRS] = jnp.zeros((FEATS, TILE), jnp.float32)

    def products(half, segment, total):
        first_pair, length, unroll = SEGMENTS[segment]

        def some(step, total):
            for j in range(unroll):
                pair = first_pair + step * unroll + j
                spot = pair * 2
                one = tbl_ref[spot >> 7, spot & (TILE - 1)]
                two = tbl_ref[spot >> 7, (spot & (TILE - 1)) + 1]
                left = jnp.concatenate(
                    [s_refs[half][(one >> 1) & (NSRC - 1)], s_refs[half][(two >> 1) & (NSRC - 1)]], axis=1)
                right = jnp.concatenate([a_ref[one >> 7], a_ref[two >> 7]], axis=1)
                value = lax.dot_general(
                    left, right, (((1,), (1,)), ((), ())), preferred_element_type=jnp.float32)
                keep = (1 - (one & 1)).astype(jnp.float32)
                total = value + total * keep
                sum_ref[half, pair] = total
            return total

        return lax.fori_loop(0, length // unroll, some, total)

    def summed(half, away, part):
        at_tile = (away + GROUPS // 2) % GROUPS * TPS + part * PART
        return [sum_ref[half, tbl_ref[4, at_tile + j]] for j in range(PART)]

    def ring(half, m, way):
        reach = 4 - (m + 1) // 2
        part = (m % 2) ^ way
        values = summed(half, reach if way == 0 else GROUPS - reach, part)
        if m >= 2:
            wait_in(ring_in.at[half, way, m - 2], ring_r.at[half, way, m - 2])
        for j in range(PART):
            value = values[j]
            if m >= 2:
                value = value + ring_in[half, way, m - 2, j].astype(jnp.float32)
            ring_out[half, way, m, j] = value.astype(jnp.bfloat16)
        send(ring_out.at[half, way, m], ring_in.at[half, way, m],
             ring_s.at[half, way, m], ring_r.at[half, way, m], to_z[way])

    def both(half, m):
        for way in range(2):
            ring(half, m, way)

    def final(half):
        for m in (5, 6):
            for way in range(2):
                wait_in(ring_in.at[half, way, m], ring_r.at[half, way, m])
        for part in range(2):
            values = summed(half, 0, part)
            for j in range(PART):
                value = values[j] + ring_in[half, part, 6, j].astype(jnp.float32)
                value = value + ring_in[half, 1 - part, 5, j].astype(jnp.float32)
                fin_ref[part * PART + j, pl.ds(half * FEATS, FEATS), :] = value

    ys = (y, yu, yd, yo)

    def hand(half, number, ref):
        send(ref, ref, sib_s.at[half, number], sib_r.at[half, number], to_sib)

    def sib_in(half):
        for number in range(16):
            k = number % 8
            rows = a_rows if number < 8 else b_rows
            wait_in(rows(half, ys[k // 2], hs[k % 2], 1 - c), sib_r.at[half, number])

    def level1(half):
        for i in range(2):
            frm = yd if i == 0 else yu
            wait_in(t_ref.at[half, frm], t_r.at[half, i])
            tile = t_ref.at[half, frm, i]
            send(tile, tile, tr_s.at[half, i], tr_r.at[half, i], to_y[i])
            for v in range(2):
                send(t_ref.at[half, frm], b_rows(half, frm, h, c),
                     xb_s.at[half, 2 - i, v], xb_r.at[half, 2 - i, v], to_x[v])
        for i in range(2):
            ref = a_rows(half, y, hs[i], c)
            wait_in(ref, xa_r.at[half, i])
            for v in range(2):
                send(ref, ref, ya_s.at[half, v, i], ya_r.at[half, v, i], to_y[v])
            hand(half, i, ref)
        for i in range(2):
            ref = b_rows(half, y, hs[i], c)
            wait_in(ref, xb_r.at[half, 0, i])
            hand(half, 8 + i, ref)

    def level2(half):
        for i in range(2):
            wait_in(t_ref.at[half, yo, i], tr_r.at[half, i])
        for i in range(2):
            send(t_ref.at[half, yo], b_rows(half, yo, h, c),
                 xb_s.at[half, 3, i], xb_r.at[half, 3, i], to_x[i])
        for i in range(2):
            for v in (i, 1 - i):
                frm = yd if v == 0 else yu
                ref = a_rows(half, frm, hs[i], c)
                wait_in(ref, ya_r.at[half, v, i])
                if i == v:
                    send(ref, ref, yr_s.at[half, i], yr_r.at[half, i], to_y[v])
                hand(half, (4 if v == 0 else 2) + i, ref)
        for n, frm in ((2, yd), (1, yu)):
            for i in range(2):
                ref = b_rows(half, frm, hs[i], c)
                wait_in(ref, xb_r.at[half, n, i])
                hand(half, 8 + 2 * n + i, ref)

    def level3(half):
        for i in range(2):
            ref = b_rows(half, yo, hs[i], c)
            wait_in(ref, xb_r.at[half, 3, i])
            hand(half, 14 + i, ref)
        for i in range(2):
            ref = a_rows(half, yo, hs[i], c)
            wait_in(ref, yr_r.at[half, i])
            hand(half, 6 + i, ref)

    level1(0)
    level1(1)
    level2(0)
    tbl_copy.wait()
    for copy in adj_copies:
        copy.wait()
    level2(1)
    level3(0)
    sib_in(0)
    nothing = jnp.zeros((FEATS, TILE), jnp.float32)
    total = products(0, 0, nothing)
    ring(0, 0, 0)
    total = products(0, 1, total)
    ring(0, 0, 1)
    level3(1)
    total = products(0, 2, total)
    both(0, 1)
    sib_in(1)
    total = products(1, 0, nothing)
    ring(1, 0, 0)
    both(0, 2)
    total = products(1, 1, total)
    ring(1, 0, 1)
    both(0, 3)
    total = products(1, 2, total)
    both(1, 1)
    both(0, 4)
    both(1, 2)
    both(0, 5)
    both(1, 3)
    both(0, 6)
    both(1, 4)
    both(1, 5)
    both(1, 6)
    final(0)
    final(1)
    for tile in range(TPS):
        value = fin_ref[tile] * inverse(tile)
        out_ref[0, pl.ds(tile * TILE, TILE), :] = jnp.transpose(value).astype(jnp.bfloat16)
    for copy in sends:
        copy.wait_send()


def shards(embed_codes, embed_exps, degrees, adjacency, block_index):
    dma = pltpu.SemaphoreType.DMA
    narrow = jnp.bfloat16
    sems = []
    for shape in ((2, 2), (2, 4, 2), (2, 2, 2), (2, 2), (2, 2), (2, 2), (2, 16), (2, 2, 7)):
        sems += [dma(shape), dma(shape)]
    return pl.pallas_call(
        kernel,
        out_shape=jax.ShapeDtypeStruct(embed_codes.shape, narrow),
        in_specs=[pl.BlockSpec(memory_space=pltpu.HBM)] * 5,
        out_specs=pl.BlockSpec(memory_space=pltpu.VMEM),
        scratch_shapes=[
            pltpu.VMEM((SLOTS + 1, TILE, TILE), narrow),
            pltpu.VMEM((NSRC, FEATS, TILE), narrow),
            pltpu.VMEM((NSRC, FEATS, TILE), narrow),
            pltpu.VMEM((2, NY, PART, FEATS, TILE), narrow),
            pltpu.VMEM((2, PART, FEATS, TILE), narrow),
            pltpu.VMEM((2, PAIRS + 1, FEATS, TILE), jnp.float32),
            pltpu.VMEM((TPS, TILE, TILE), jnp.float32),
            pltpu.VMEM((8, TILE), jnp.int32),
            pltpu.SMEM((8, TILE), jnp.int32),
            pltpu.VMEM(embed_codes.shape, embed_codes.dtype),
            pltpu.SMEM(embed_exps.shape, embed_exps.dtype),
            pltpu.VMEM(degrees.shape, degrees.dtype),
            pltpu.VMEM(block_index.shape, block_index.dtype),
            pltpu.VMEM((2, 2, 7, PART, FEATS, TILE), narrow),
            pltpu.VMEM((2, 2, 7, PART, FEATS, TILE), narrow),
            dma((4,)), dma((ADJ_PIECES,)), dma(()),
            *sems,
        ],
        compiler_params=pltpu.CompilerParams(
            collective_id=0, has_side_effects=True, vmem_limit_bytes=67_043_328
        ),
    )(embed_codes, embed_exps, degrees, adjacency.reshape(adjacency.shape[1:]), block_index)


def solution(mesh):
    placed = (
        P("side", ("grp", "blk"), None),
        P("side", ("grp", "blk")),
        P("side", ("grp", "blk")),
        P("side", ("grp", "blk"), None, None),
        P("side", None, ("grp", "blk")),
    )
    return jax.shard_map(
        shards,
        mesh=mesh,
        in_specs=placed,
        out_specs=P("side", ("grp", "blk"), None),
        check_vma=False,
    )
```

```python
import jax
import jax.numpy as jnp
from jax import lax
from jax.experimental import pallas as pl
from jax.experimental.pallas import tpu as pltpu
from jax.sharding import PartitionSpec as P

MESH = pl.DeviceIdType.MESH
TILE = 128
TPS = 4
ROWS = TILE * TPS
PART = TPS // 2
NY, NH, NC = 4, 2, 2
GROUPS = 8
DST = 32
SLOTS = 384
ADJ_PIECES = 8
PAIRS = (SLOTS + DST) // 2
NSRC = 64
SEGMENTS = (0, 32, 64, 96, 128, 208)


def kernel(
    codes_hbm, exps_hbm, deg_hbm, adj_ref, index_hbm, out_ref,
    a_ref, s_ref, t_ref, own_ref, sum_ref, inv_ref, tblv_ref, tbl_ref,
    codes_ref, exps_ref, deg_ref, index_ref,
    ring_out, ring_in,
    in_sem, adj_sem, tbl_sem,
    xa_s, xa_r, xb_s, xb_r, xc_s, xc_r, ya_s, ya_r, yr_s, yr_r, t_s, t_r, tr_s, tr_r,
    sib_s, sib_r, ring_s, ring_r,
):
    side = lax.axis_index("side")
    grp = lax.axis_index("grp")
    blk = lax.axis_index("blk")
    y, h, c = blk // (NH * NC), (blk // NC) % NH, blk % NC
    other = 1 - side

    def at(yy, hh, cc):
        return (yy * NH + hh) * NC + cc

    yu, yd, yo = (y + 1) % NY, (y + NY - 1) % NY, (y + 2) % NY
    gu, gd = (grp + 1) % GROUPS, (grp + GROUPS - 1) % GROUPS
    hs = (h, 1 - h)
    to_x = [(other, grp, at(y, hh, c)) for hh in hs]
    to_y = [(side, grp, at(yu, h, c)), (side, grp, at(yd, h, c))]
    to_sib = (side, grp, at(y, h, 1 - c))
    to_z = [(side, gu, blk), (side, gd, blk)]

    barrier = pltpu.get_barrier_semaphore()
    partners = [*to_x, *to_y, to_sib, *to_z]
    for target in partners:
        pl.semaphore_signal(barrier, inc=1, device_id=target, device_id_type=MESH)

    small = [
        pltpu.make_async_copy(src, dst, in_sem.at[i])
        for i, (src, dst) in enumerate((
            (exps_hbm, exps_ref), (deg_hbm, deg_ref), (codes_hbm, codes_ref), (index_hbm, index_ref)))
    ]
    for copy in small:
        copy.start()
    adj_copies = []
    per = SLOTS // ADJ_PIECES
    for piece in range(ADJ_PIECES):
        cut = pl.ds(piece * per, per)
        copy = pltpu.make_async_copy(adj_ref.at[cut], a_ref.at[cut], adj_sem.at[piece])
        copy.start()
        adj_copies.append(copy)

    def column(row):
        return jnp.transpose(jnp.broadcast_to(row, (TILE, TILE)))

    for copy in small[:3]:
        copy.wait()
    for tile in range(TPS):
        lanes = deg_ref[0:1, tile * TILE:(tile + 1) * TILE].astype(jnp.float32)
        inverse = column(lax.rsqrt(lanes))
        inv_ref[pl.ds(tile * TILE, TILE), :] = inverse
        power = jnp.exp2(jnp.full((TILE, TILE), exps_ref[0, tile], jnp.int32).astype(jnp.float32))
        rows = codes_ref[0, pl.ds(tile * TILE, TILE), :].astype(jnp.float32)
        rows = (rows * power * inverse).astype(jnp.bfloat16)
        if tile < TPS // 2:
            own_ref[tile] = rows
        else:
            t_ref[y, tile - TPS // 2] = rows

    pl.semaphore_wait(barrier, len(partners))

    sends = []

    def send(src, dst, ssem, rsem, target):
        copy = pltpu.make_async_remote_copy(
            src_ref=src, dst_ref=dst, send_sem=ssem, recv_sem=rsem,
            device_id=target, device_id_type=MESH,
        )
        copy.start()
        sends.append(copy)

    def wait_in(dst, rsem):
        pltpu.make_async_copy(dst, dst, rsem).wait()

    def tiles(yy, hh, cc, first, count):
        return s_ref.at[pl.ds(at(yy, hh, cc) * TPS + first, count)]

    for j in range(PART):
        for i in range(2):
            send(own_ref.at[j], s_ref.at[at(y, h, c) * TPS + j], xa_s.at[j, i], xa_r.at[j, i], to_x[i])
            k = i ^ j
            send(t_ref.at[y, k], t_ref.at[y, k], t_s.at[i, k], t_r.at[i, k], to_y[i])
    for i in range(2):
        send(t_ref.at[y], tiles(y, h, c, PART, PART), xb_s.at[0, i], xb_r.at[0, i], to_x[i])

    small[3].wait()
    sub = lax.broadcasted_iota(jnp.int32, (TILE, TILE), 0)
    lane = lax.broadcasted_iota(jnp.int32, (TILE, TILE), 1)
    lane_row = lax.broadcasted_iota(jnp.int32, (1, TILE), 1)
    cuts = range(SLOTS // TILE)

    def down(mask, value=1):
        return jnp.sum(jnp.where(mask, value, 0), axis=0, keepdims=True)

    target = [index_ref[0, 0:1, j * TILE:(j + 1) * TILE] for j in cuts]
    source = [index_ref[0, 1:2, j * TILE:(j + 1) * TILE] for j in cuts]
    used = [q < NSRC for q in source]
    shift = (GROUPS + GROUPS // 2 - grp) * TPS

    def order(t):
        group = (t + shift) & (DST - TPS)
        return group + ((t & 1) << 1) + ((t >> 1) & 1)

    key = [jnp.where(u, order(t), DST) for u, t in zip(used, target)]
    key_col = [column(t) for t in key]
    count = sum(down(k == lane) for k in key_col)
    padded = jnp.where(lane_row < DST, (count + 1) & ~1, 0)
    padded_col = column(padded)
    begin = down(sub < lane, padded_col)
    begin_col = column(begin)
    place_col, code_col = [], []
    for j in cuts:
        rank = down((key_col[j] == key[j]) & (sub < lane))
        for i in range(j):
            rank = rank + down(key_col[i] == key[j])
        place = down(sub < key[j], padded_col) + rank
        place_col.append(column(jnp.where(used[j], place, 8 * TILE)))
        code_col.append(((j * TILE + sub) * NSRC + column(source[j])) * 2)
    for r in range(4):
        spot = lane + r * TILE
        code = jnp.full((TILE, TILE), -1, jnp.int32)
        for j in cuts:
            code = jnp.where(place_col[j] == spot, code_col[j], code)
        code = jnp.max(code, axis=0, keepdims=True)
        first = down((begin_col == spot) & (padded_col > 0))
        tblv_ref[r:r + 1, :] = jnp.where(code < 0, SLOTS * NSRC * 2, code) + first
    tblv_ref[4:5, :] = jnp.where(padded > 0, ((begin + padded) >> 1) - 1, PAIRS)
    tbl_copy = pltpu.make_async_copy(tblv_ref, tbl_ref, tbl_sem)
    tbl_copy.start()
    a_ref[SLOTS] = jnp.zeros((TILE, TILE), jnp.bfloat16)
    sum_ref[PAIRS] = jnp.zeros((TILE, TILE), jnp.float32)

    def products(segment, total):
        for pair in range(SEGMENTS[segment], SEGMENTS[segment + 1]):
            row, spot = pair // (TILE // 2), pair % (TILE // 2) * 2
            one, two = tbl_ref[row, spot], tbl_ref[row, spot + 1]
            left = jnp.concatenate([a_ref[one >> 7], a_ref[two >> 7]], axis=1)
            right = jnp.concatenate(
                [s_ref[(one >> 1) & (NSRC - 1)], s_ref[(two >> 1) & (NSRC - 1)]], axis=0)
            value = jnp.dot(left, right, preferred_element_type=jnp.float32)
            keep = (1 - (one & 1)).astype(jnp.float32)
            total = value + total * keep
            sum_ref[pair] = total
        return total

    def summed(away, part, j):
        return sum_ref[tbl_ref[4, (away + GROUPS // 2) % GROUPS * TPS + j * PART + part]]

    def ring(m, way, j):
        reach = 4 - (m + 1) // 2
        value = summed(reach if way == 0 else GROUPS - reach, (m % 2) ^ way, j)
        if m >= 2:
            wait_in(ring_in.at[way, m - 2, j], ring_r.at[way, m - 2, j])
            value = value + ring_in[way, m - 2, j].astype(jnp.float32)
        ring_out[way, m, j] = value.astype(jnp.bfloat16)
        send(ring_out.at[way, m, j], ring_in.at[way, m, j],
             ring_s.at[way, m, j], ring_r.at[way, m, j], to_z[way])

    expected = []

    def hand(yy, i, first, count):
        number = len(expected)
        ref = tiles(yy, hs[i], c, first, count)
        send(ref, ref, sib_s.at[number], sib_r.at[number], to_sib)
        expected.append(tiles(yy, hs[i], 1 - c, first, count))

    def wait_tiles(yy, i, first, count, rsem):
        ref = tiles(yy, hs[i], c, first, count)
        wait_in(ref, rsem)
        return ref

    near = (yd, yu)
    for i in range(2):
        tile = t_ref.at[near[i], i]
        wait_in(tile, t_r.at[i, i])
        send(tile, tile, tr_s.at[i], tr_r.at[i], to_y[i])

    def pass_on(j, i, v):
        ref = tiles(y, hs[i], c, j, 1)
        send(ref, ref, ya_s.at[v, i, j], ya_r.at[v, i, j], to_y[v])

    for i in range(2):
        wait_tiles(y, i, 0, 1, xa_r.at[0, i])
        pass_on(0, i, i)
    for i in range(2):
        wait_in(t_ref.at[near[i], 1 - i], t_r.at[i, 1 - i])
        for v in range(2):
            send(t_ref.at[near[i]], tiles(near[i], h, c, PART, PART),
                 xb_s.at[2 - i, v], xb_r.at[2 - i, v], to_x[v])
    for i in range(2):
        wait_tiles(y, i, 1, 1, xa_r.at[1, i])
        pass_on(1, i, i)
    for j in range(PART):
        for i in range(2):
            pass_on(j, i, 1 - i)
    for i in range(2):
        hand(y, i, 0, PART)
    for i in range(2):
        wait_tiles(y, i, PART, PART, xb_r.at[0, i])
        hand(y, i, PART, PART)
    for i in range(2):
        wait_in(t_ref.at[yo, i], tr_r.at[i])
        for v in range(2):
            send(t_ref.at[yo, i], s_ref.at[at(yo, h, c) * TPS + PART + i],
                 xc_s.at[i, v], xc_r.at[i, v], to_x[v])
    for j in range(PART):
        for i in range(2):
            ref = wait_tiles(near[i], i, j, 1, ya_r.at[i, i, j])
            send(ref, ref, yr_s.at[i, j], yr_r.at[i, j], to_y[i])
    for i in range(2):
        hand(near[i], i, 0, PART)
    for i in range(2):
        for v in range(2):
            wait_tiles(near[i], v, PART, PART, xb_r.at[2 - i, v])
            hand(near[i], v, PART, PART)
    for i in range(2):
        for j in range(PART):
            wait_tiles(near[i], 1 - i, j, 1, ya_r.at[i, 1 - i, j])
        hand(near[i], 1 - i, 0, PART)
    for j in range(PART):
        for i in range(2):
            wait_tiles(yo, i, PART + j, 1, xc_r.at[j, i])
            hand(yo, i, PART + j, 1)
        for i in range(2):
            wait_tiles(yo, i, j, 1, yr_r.at[i, j])
            hand(yo, i, j, 1)
    tbl_copy.wait()
    for copy in adj_copies:
        copy.wait()
    for number, ref in enumerate(expected):
        wait_in(ref, sib_r.at[number])

    total = jnp.zeros((TILE, TILE), jnp.float32)
    for segment in range(TPS):
        total = products(segment, total)
        ring(0, segment % 2, segment // 2)
    products(TPS, total)
    for m in range(1, 7):
        for j in range(PART):
            for way in range(2):
                ring(m, way, j)
    for j in range(PART):
        for m, way in ((5, 0), (5, 1), (6, 0), (6, 1)):
            wait_in(ring_in.at[way, m, j], ring_r.at[way, m, j])
        for part in range(2):
            value = summed(0, part, j) + ring_in[part, 6, j].astype(jnp.float32)
            value = value + ring_in[1 - part, 5, j].astype(jnp.float32)
            cut = pl.ds((part * PART + j) * TILE, TILE)
            out_ref[0, cut, :] = (value * inv_ref[cut, :]).astype(jnp.bfloat16)
    for copy in sends:
        copy.wait_send()


def shards(embed_codes, embed_exps, degrees, adjacency, block_index):
    width = embed_codes.shape[2]
    dma = pltpu.SemaphoreType.DMA
    vmem = pl.BlockSpec(memory_space=pltpu.VMEM)
    sems = []
    for shape in ((2, 2), (3, 2), (2, 2), (2, 2, 2), (2, 2), (2, 2), (2,), (20,), (2, 7, PART)):
        sems += [dma(shape), dma(shape)]
    return pl.pallas_call(
        kernel,
        out_shape=jax.ShapeDtypeStruct(embed_codes.shape, jnp.bfloat16),
        in_specs=[pl.BlockSpec(memory_space=pltpu.HBM)] * 5,
        out_specs=vmem,
        scratch_shapes=[
            pltpu.VMEM((SLOTS + 1, TILE, TILE), jnp.bfloat16),
            pltpu.VMEM((NSRC, TILE, width), jnp.bfloat16),
            pltpu.VMEM((NY, TPS // 2, TILE, width), jnp.bfloat16),
            pltpu.VMEM((TPS // 2, TILE, width), jnp.bfloat16),
            pltpu.VMEM((PAIRS + 1, TILE, width), jnp.float32),
            pltpu.VMEM((ROWS, width), jnp.float32),
            pltpu.VMEM((8, TILE), jnp.int32),
            pltpu.SMEM((8, TILE), jnp.int32),
            pltpu.VMEM(embed_codes.shape, embed_codes.dtype),
            pltpu.SMEM(embed_exps.shape, embed_exps.dtype),
            pltpu.VMEM(degrees.shape, degrees.dtype),
            pltpu.VMEM(block_index.shape, block_index.dtype),
            pltpu.VMEM((2, 7, PART, TILE, width), jnp.bfloat16),
            pltpu.VMEM((2, 7, PART, TILE, width), jnp.bfloat16),
            dma((4,)), dma((ADJ_PIECES,)), dma(()),
            *sems,
        ],
        compiler_params=pltpu.CompilerParams(
            collective_id=0, has_side_effects=True, vmem_limit_bytes=67_043_328
        ),
    )(embed_codes, embed_exps, degrees, adjacency.reshape(adjacency.shape[1:]), block_index)


def solution(mesh):
    placed = (
        P("side", ("grp", "blk"), None),
        P("side", ("grp", "blk")),
        P("side", ("grp", "blk")),
        P("side", ("grp", "blk"), None, None),
        P("side", None, ("grp", "blk")),
    )
    return jax.shard_map(
        shards,
        mesh=mesh,
        in_specs=placed,
        out_specs=P("side", ("grp", "blk"), None),
        check_vma=False,
    )
```

```python
import jax
import jax.numpy as jnp
from jax import lax
from jax.experimental import pallas as pl
from jax.experimental.pallas import tpu as pltpu
from jax.sharding import PartitionSpec as P

MESH = pl.DeviceIdType.MESH
TILE = 128
TPS = 4
ROWS = TILE * TPS
PART = TPS // 2
NY, NH, NC = 4, 2, 2
GROUPS = 8
DST = 32
SLOTS = 384
ADJ_PIECES = 2
PAIRS = (SLOTS + DST) // 2
NSRC = 64
SEGMENTS = (0, 32, 64, 96, 128, 160, 192, 208)


def kernel(
    codes_hbm, exps_hbm, deg_hbm, adj_ref, index_hbm, out_ref,
    a_ref, s_ref, t_ref, own_ref, sum_ref, inv_ref, tblv_ref, tbl_ref,
    codes_ref, exps_ref, deg_ref, index_ref,
    ring_out, ring_in,
    in_sem, adj_sem, tbl_sem,
    xa_s, xa_r, xb_s, xb_r, xc_s, xc_r, ya_s, ya_r, yr_s, yr_r, t_s, t_r, tr_s, tr_r,
    sib_s, sib_r, ring_s, ring_r,
):
    side = lax.axis_index("side")
    grp = lax.axis_index("grp")
    blk = lax.axis_index("blk")
    y, h, c = blk // (NH * NC), (blk // NC) % NH, blk % NC
    other = 1 - side

    def at(yy, hh, cc):
        return (yy * NH + hh) * NC + cc

    yu, yd, yo = (y + 1) % NY, (y + NY - 1) % NY, (y + 2) % NY
    gu, gd = (grp + 1) % GROUPS, (grp + GROUPS - 1) % GROUPS
    hs = (h, 1 - h)
    to_x = [(other, grp, at(y, hh, c)) for hh in hs]
    to_y = [(side, grp, at(yu, h, c)), (side, grp, at(yd, h, c))]
    to_sib = (side, grp, at(y, h, 1 - c))
    to_z = [(side, gu, blk), (side, gd, blk)]
    to_z2 = [(side, (grp + 2) % GROUPS, blk), (side, (grp + GROUPS - 2) % GROUPS, blk)]

    small = [
        pltpu.make_async_copy(src, dst, in_sem.at[i])
        for i, (src, dst) in enumerate((
            (exps_hbm, exps_ref), (deg_hbm, deg_ref), (codes_hbm, codes_ref), (index_hbm, index_ref)))
    ]
    for copy in small:
        copy.start()
    barrier = pltpu.get_barrier_semaphore()
    partners = [*to_z2, *to_z, *to_x, *to_y, to_sib]
    for target in partners:
        pl.semaphore_signal(barrier, inc=1, device_id=target, device_id_type=MESH)

    def column(row):
        return jnp.transpose(jnp.broadcast_to(row, (TILE, TILE)))

    for copy in small[:3]:
        copy.wait()
    for tile in range(TPS):
        lanes = deg_ref[0:1, tile * TILE:(tile + 1) * TILE].astype(jnp.float32)
        inverse = column(lax.rsqrt(lanes))
        inv_ref[pl.ds(tile * TILE, TILE), :] = inverse
        power = jnp.exp2(jnp.full((TILE, TILE), exps_ref[0, tile], jnp.int32).astype(jnp.float32))
        rows = codes_ref[0, pl.ds(tile * TILE, TILE), :].astype(jnp.float32)
        rows = (rows * power * inverse).astype(jnp.bfloat16)
        if tile < TPS // 2:
            own_ref[tile] = rows
        else:
            t_ref[y, tile - TPS // 2] = rows

    pl.semaphore_wait(barrier, len(partners))

    sends = []

    def send(src, dst, ssem, rsem, target):
        copy = pltpu.make_async_remote_copy(
            src_ref=src, dst_ref=dst, send_sem=ssem, recv_sem=rsem,
            device_id=target, device_id_type=MESH,
        )
        copy.start()
        sends.append(copy)

    def settle(keep=0):
        while len(sends) > keep:
            sends.pop(0).wait_send()

    def wait_in(dst, rsem):
        pltpu.make_async_copy(dst, dst, rsem).wait()

    def tiles(yy, hh, cc, first, count):
        return s_ref.at[pl.ds(at(yy, hh, cc) * TPS + first, count)]

    for j in range(PART):
        for i in range(2):
            send(own_ref.at[j], s_ref.at[at(y, h, c) * TPS + j], xa_s.at[j, i], xa_r.at[j, i], to_x[i])
            k = i ^ j
            send(t_ref.at[y, k], t_ref.at[y, k], t_s.at[i, k], t_r.at[i, k], to_y[i])
    for i in range(2):
        send(t_ref.at[y], tiles(y, h, c, PART, PART), xb_s.at[0, i], xb_r.at[0, i], to_x[i])

    adj_copies = []
    per = SLOTS // ADJ_PIECES
    for piece in range(ADJ_PIECES):
        cut = pl.ds(piece * per, per)
        copy = pltpu.make_async_copy(adj_ref.at[cut], a_ref.at[cut], adj_sem.at[piece])
        copy.start()
        adj_copies.append(copy)

    small[3].wait()
    sub = lax.broadcasted_iota(jnp.int32, (TILE, TILE), 0)
    lane = lax.broadcasted_iota(jnp.int32, (TILE, TILE), 1)
    lane_row = lax.broadcasted_iota(jnp.int32, (1, TILE), 1)
    cuts = range(SLOTS // TILE)

    def down(mask, value=1):
        return jnp.sum(jnp.where(mask, value, 0), axis=0, keepdims=True)

    target = [index_ref[0, 0:1, j * TILE:(j + 1) * TILE] for j in cuts]
    source = [index_ref[0, 1:2, j * TILE:(j + 1) * TILE] for j in cuts]
    used = [q < NSRC for q in source]
    shift = (GROUPS + GROUPS // 2 - grp) * TPS

    def order(t):
        group, tile = ((t + shift) & (DST - 1)) >> 2, t & 3
        turn = ((tile & 1) << 1) + (tile >> 1)
        near = jnp.where(group == 1, TPS + 2 * turn, TPS + 1 + 2 * (turn ^ 1))
        rest = 3 * TPS + (group - 2) * TPS + tile
        return jnp.where(group == 0, turn, jnp.where((group == 1) | (group == 7), near, rest))

    key = [jnp.where(u, order(t), DST) for u, t in zip(used, target)]
    key_col = [column(t) for t in key]
    count = sum(down(k == lane) for k in key_col)
    padded = jnp.where(lane_row < DST, (count + 1) & ~1, 0)
    padded_col = column(padded)
    begin = down(sub < lane, padded_col)
    begin_col = column(begin)
    place_col, code_col = [], []
    for j in cuts:
        rank = down((key_col[j] == key[j]) & (sub < lane))
        for i in range(j):
            rank = rank + down(key_col[i] == key[j])
        place = down(sub < key[j], padded_col) + rank
        place_col.append(column(jnp.where(used[j], place, 8 * TILE)))
        code_col.append(((j * TILE + sub) * NSRC + column(source[j])) * 2)
    for r in range(4):
        spot = lane + r * TILE
        code = jnp.full((TILE, TILE), -1, jnp.int32)
        for j in cuts:
            code = jnp.where(place_col[j] == spot, code_col[j], code)
        code = jnp.max(code, axis=0, keepdims=True)
        first = down((begin_col == spot) & (padded_col > 0))
        tblv_ref[r:r + 1, :] = jnp.where(code < 0, SLOTS * NSRC * 2, code) + first
    tblv_ref[4:5, :] = jnp.where(padded > 0, ((begin + padded) >> 1) - 1, PAIRS)
    tbl_copy = pltpu.make_async_copy(tblv_ref, tbl_ref, tbl_sem)
    tbl_copy.start()
    a_ref[SLOTS] = jnp.zeros((TILE, TILE), jnp.bfloat16)
    sum_ref[PAIRS] = jnp.zeros((TILE, TILE), jnp.float32)

    def products(segment, total):
        for pair in range(SEGMENTS[segment], SEGMENTS[segment + 1]):
            row, spot = pair // (TILE // 2), pair % (TILE // 2) * 2
            one, two = tbl_ref[row, spot], tbl_ref[row, spot + 1]
            left = jnp.concatenate([a_ref[one >> 7], a_ref[two >> 7]], axis=1)
            right = jnp.concatenate(
                [s_ref[(one >> 1) & (NSRC - 1)], s_ref[(two >> 1) & (NSRC - 1)]], axis=0)
            value = jnp.dot(left, right, preferred_element_type=jnp.float32)
            keep = (1 - (one & 1)).astype(jnp.float32)
            total = value + total * keep
            sum_ref[pair] = total
        return total

    def summed(away, part, j):
        group, turn = (away + GROUPS // 2) % GROUPS, j * PART + part
        if group == 0:
            spot = turn
        elif group == 1:
            spot = TPS + 2 * turn
        elif group == 7:
            spot = TPS + 1 + 2 * (turn ^ 1)
        else:
            spot = 3 * TPS + (group - 2) * TPS + part * PART + j
        return sum_ref[tbl_ref[4, spot]]

    def ring(m, way, j):
        reach = 4 - (m + 1) // 2
        value = summed(reach if way == 0 else GROUPS - reach, (m % 2) ^ way, j)
        for n in {3: (1,), 4: (0, 2), 5: (3,), 6: (4,)}.get(m, ()):
            wait_in(ring_in.at[way, n, j], ring_r.at[way, n, j])
            value = value + ring_in[way, n, j].astype(jnp.float32)
        ring_out[way, m, j] = value.astype(jnp.bfloat16)
        send(ring_out.at[way, m, j], ring_in.at[way, m, j],
             ring_s.at[way, m, j], ring_r.at[way, m, j], to_z2[way] if m == 0 else to_z[way])

    expected = []

    def hand(yy, i, first, count):
        number = len(expected)
        ref = tiles(yy, hs[i], c, first, count)
        send(ref, ref, sib_s.at[number], sib_r.at[number], to_sib)
        expected.append(tiles(yy, hs[i], 1 - c, first, count))

    def wait_tiles(yy, i, first, count, rsem):
        ref = tiles(yy, hs[i], c, first, count)
        wait_in(ref, rsem)
        return ref

    near = (yd, yu)
    for i in range(2):
        tile = t_ref.at[near[i], i]
        wait_in(tile, t_r.at[i, i])
        send(tile, tile, tr_s.at[i], tr_r.at[i], to_y[i])

    def pass_on(j, i, v):
        ref = tiles(y, hs[i], c, j, 1)
        send(ref, ref, ya_s.at[v, i, j], ya_r.at[v, i, j], to_y[v])

    for i in range(2):
        wait_tiles(y, i, 0, 1, xa_r.at[0, i])
        pass_on(0, i, i)
    for i in range(2):
        wait_in(t_ref.at[near[i], 1 - i], t_r.at[i, 1 - i])
        for v in range(2):
            send(t_ref.at[near[i]], tiles(near[i], h, c, PART, PART),
                 xb_s.at[2 - i, v], xb_r.at[2 - i, v], to_x[v])
    for i in range(2):
        wait_tiles(y, i, 1, 1, xa_r.at[1, i])
        pass_on(1, i, i)
    for j in range(PART):
        for i in range(2):
            pass_on(j, i, 1 - i)
    for i in range(2):
        hand(y, i, 0, PART)
    for i in range(2):
        wait_tiles(y, i, PART, PART, xb_r.at[0, i])
        hand(y, i, PART, PART)
    for i in range(2):
        wait_in(t_ref.at[yo, i], tr_r.at[i])
        for v in range(2):
            send(t_ref.at[yo, i], s_ref.at[at(yo, h, c) * TPS + PART + i],
                 xc_s.at[i, v], xc_r.at[i, v], to_x[v])
    for j in range(PART):
        for i in range(2):
            ref = wait_tiles(near[i], i, j, 1, ya_r.at[i, i, j])
            send(ref, ref, yr_s.at[i, j], yr_r.at[i, j], to_y[i])
    for i in range(2):
        hand(near[i], i, 0, PART)
    for i in range(2):
        for v in range(2):
            wait_tiles(near[i], v, PART, PART, xb_r.at[2 - i, v])
            hand(near[i], v, PART, PART)
    for i in range(2):
        for j in range(PART):
            wait_tiles(near[i], 1 - i, j, 1, ya_r.at[i, 1 - i, j])
        hand(near[i], 1 - i, 0, PART)
    for j in range(PART):
        for i in range(2):
            wait_tiles(yo, i, PART + j, 1, xc_r.at[j, i])
            hand(yo, i, PART + j, 1)
        for i in range(2):
            wait_tiles(yo, i, j, 1, yr_r.at[i, j])
            hand(yo, i, j, 1)
    tbl_copy.wait()
    for copy in adj_copies:
        copy.wait()
    for number, ref in enumerate(expected):
        wait_in(ref, sib_r.at[number])

    total = jnp.zeros((TILE, TILE), jnp.float32)
    early = ((0, 0, 0), (0, 1, 0), (0, 0, 1), (0, 1, 1), (1, 1, 0), (1, 0, 0))
    for segment, piece in enumerate(early):
        total = products(segment, total)
        ring(*piece)
    products(len(early), total)
    for m, j in ((2, 0), (1, 1), (2, 1)):
        for way in range(2):
            ring(m, way, j)
    for m, j in ((3, 0), (4, 0), (3, 1), (4, 1), (5, 0), (6, 0), (5, 1), (6, 1)):
        for way in range(2):
            ring(m, way, j)
    for j in range(PART):
        for m, way in ((5, 0), (5, 1), (6, 0), (6, 1)):
            wait_in(ring_in.at[way, m, j], ring_r.at[way, m, j])
        for part in range(2):
            value = summed(0, part, j) + ring_in[part, 6, j].astype(jnp.float32)
            value = value + ring_in[1 - part, 5, j].astype(jnp.float32)
            cut = pl.ds((part * PART + j) * TILE, TILE)
            out_ref[0, cut, :] = (value * inv_ref[cut, :]).astype(jnp.bfloat16)
    settle()


def shards(embed_codes, embed_exps, degrees, adjacency, block_index):
    width = embed_codes.shape[2]
    dma = pltpu.SemaphoreType.DMA
    vmem = pl.BlockSpec(memory_space=pltpu.VMEM)
    sems = []
    for shape in ((2, 2), (3, 2), (2, 2), (2, 2, 2), (2, 2), (2, 2), (2,), (20,), (2, 7, PART)):
        sems += [dma(shape), dma(shape)]
    return pl.pallas_call(
        kernel,
        out_shape=jax.ShapeDtypeStruct(embed_codes.shape, jnp.bfloat16),
        in_specs=[pl.BlockSpec(memory_space=pltpu.HBM)] * 5,
        out_specs=vmem,
        scratch_shapes=[
            pltpu.VMEM((SLOTS + 1, TILE, TILE), jnp.bfloat16),
            pltpu.VMEM((NSRC, TILE, width), jnp.bfloat16),
            pltpu.VMEM((NY, TPS // 2, TILE, width), jnp.bfloat16),
            pltpu.VMEM((TPS // 2, TILE, width), jnp.bfloat16),
            pltpu.VMEM((PAIRS + 1, TILE, width), jnp.float32),
            pltpu.VMEM((ROWS, width), jnp.float32),
            pltpu.VMEM((8, TILE), jnp.int32),
            pltpu.SMEM((8, TILE), jnp.int32),
            pltpu.VMEM(embed_codes.shape, embed_codes.dtype),
            pltpu.SMEM(embed_exps.shape, embed_exps.dtype),
            pltpu.VMEM(degrees.shape, degrees.dtype),
            pltpu.VMEM(block_index.shape, block_index.dtype),
            pltpu.VMEM((2, 7, PART, TILE, width), jnp.bfloat16),
            pltpu.VMEM((2, 7, PART, TILE, width), jnp.bfloat16),
            dma((4,)), dma((ADJ_PIECES,)), dma(()),
            *sems,
        ],
        compiler_params=pltpu.CompilerParams(
            collective_id=0, has_side_effects=True, vmem_limit_bytes=67_043_328
        ),
    )(embed_codes, embed_exps, degrees, adjacency.reshape(adjacency.shape[1:]), block_index)


def solution(mesh):
    placed = (
        P("side", ("grp", "blk"), None),
        P("side", ("grp", "blk")),
        P("side", ("grp", "blk")),
        P("side", ("grp", "blk"), None, None),
        P("side", None, ("grp", "blk")),
    )
    return jax.shard_map(
        shards,
        mesh=mesh,
        in_specs=placed,
        out_specs=P("side", ("grp", "blk"), None),
        check_vma=False,
    )
```

```python
import jax
import jax.numpy as jnp
from jax import lax
from jax.experimental import pallas as pl
from jax.experimental.pallas import tpu as pltpu
from jax.sharding import PartitionSpec as P

MESH = pl.DeviceIdType.MESH
TILE = 128
TPS = 4
ROWS = TILE * TPS
PART = TPS // 2
NY, NH, NC = 4, 2, 2
GROUPS = 8
DST = 32
SLOTS = 384
ADJ_PIECES = 2
PAIRS = (SLOTS + DST) // 2
NSRC = 64
SEGMENTS = (0, 32, 64, 96, 128, 160, 192, 208)


def kernel(
    codes_hbm, exps_hbm, deg_hbm, adj_ref, index_hbm, out_ref,
    a_ref, s_ref, t_ref, own_ref, sum_ref, inv_ref, tblv_ref, tbl_ref,
    codes_ref, exps_ref, deg_ref, index_ref,
    ring_out, ring_in,
    in_sem, adj_sem, tbl_sem,
    xa_s, xa_r, xb_s, xb_r, xc_s, xc_r, ya_s, ya_r, yr_s, yr_r, t_s, t_r, tr_s, tr_r,
    sib_s, sib_r, ring_s, ring_r,
):
    side = lax.axis_index("side")
    grp = lax.axis_index("grp")
    blk = lax.axis_index("blk")
    y, h, c = blk // (NH * NC), (blk // NC) % NH, blk % NC
    other = 1 - side

    def at(yy, hh, cc):
        return (yy * NH + hh) * NC + cc

    yu, yd, yo = (y + 1) % NY, (y + NY - 1) % NY, (y + 2) % NY
    gu, gd = (grp + 1) % GROUPS, (grp + GROUPS - 1) % GROUPS
    hs = (h, 1 - h)
    to_x = [(other, grp, at(y, hh, c)) for hh in hs]
    to_y = [(side, grp, at(yu, h, c)), (side, grp, at(yd, h, c))]
    to_sib = (side, grp, at(y, h, 1 - c))
    to_z = [(side, gu, blk), (side, gd, blk)]
    to_z2 = [(side, (grp + 2) % GROUPS, blk), (side, (grp + GROUPS - 2) % GROUPS, blk)]

    small = [
        pltpu.make_async_copy(src, dst, in_sem.at[i])
        for i, (src, dst) in enumerate((
            (exps_hbm, exps_ref), (deg_hbm, deg_ref), (codes_hbm, codes_ref), (index_hbm, index_ref)))
    ]
    for copy in small:
        copy.start()
    barrier = pltpu.get_barrier_semaphore()
    partners = [*to_z2, *to_z, *to_x, *to_y, to_sib]
    for target in partners:
        pl.semaphore_signal(barrier, inc=1, device_id=target, device_id_type=MESH)

    def column(row):
        return jnp.transpose(jnp.broadcast_to(row, (TILE, TILE)))

    for copy in small[:3]:
        copy.wait()
    for tile in range(TPS):
        lanes = deg_ref[0:1, tile * TILE:(tile + 1) * TILE].astype(jnp.float32)
        inverse = column(lax.rsqrt(lanes))
        inv_ref[pl.ds(tile * TILE, TILE), :] = inverse
        power = jnp.exp2(jnp.full((TILE, TILE), exps_ref[0, tile], jnp.int32).astype(jnp.float32))
        rows = codes_ref[0, pl.ds(tile * TILE, TILE), :].astype(jnp.float32)
        rows = (rows * power * inverse).astype(jnp.bfloat16)
        if tile < TPS // 2:
            own_ref[tile] = rows
        else:
            t_ref[y, tile - TPS // 2] = rows

    pl.semaphore_wait(barrier, len(partners))

    sends = []

    def send(src, dst, ssem, rsem, target):
        copy = pltpu.make_async_remote_copy(
            src_ref=src, dst_ref=dst, send_sem=ssem, recv_sem=rsem,
            device_id=target, device_id_type=MESH,
        )
        copy.start()
        sends.append(copy)

    def settle(keep=0):
        while len(sends) > keep:
            sends.pop(0).wait_send()

    def wait_in(dst, rsem):
        pltpu.make_async_copy(dst, dst, rsem).wait()

    def tiles(yy, hh, cc, first, count):
        return s_ref.at[pl.ds(at(yy, hh, cc) * TPS + first, count)]

    for j in range(PART):
        for i in range(2):
            send(own_ref.at[j], s_ref.at[at(y, h, c) * TPS + j], xa_s.at[j, i], xa_r.at[j, i], to_x[i])
            k = i ^ j
            send(t_ref.at[y, k], t_ref.at[y, k], t_s.at[i, k], t_r.at[i, k], to_y[i])
    for i in range(2):
        send(t_ref.at[y], tiles(y, h, c, PART, PART), xb_s.at[0, i, 0], xb_r.at[0, i, 0], to_x[i])

    adj_copies = []
    per = SLOTS // ADJ_PIECES
    for piece in range(ADJ_PIECES):
        cut = pl.ds(piece * per, per)
        copy = pltpu.make_async_copy(adj_ref.at[cut], a_ref.at[cut], adj_sem.at[piece])
        copy.start()
        adj_copies.append(copy)

    small[3].wait()
    sub = lax.broadcasted_iota(jnp.int32, (TILE, TILE), 0)
    lane = lax.broadcasted_iota(jnp.int32, (TILE, TILE), 1)
    lane_row = lax.broadcasted_iota(jnp.int32, (1, TILE), 1)
    cuts = range(SLOTS // TILE)

    def down(mask, value=1):
        return jnp.sum(jnp.where(mask, value, 0), axis=0, keepdims=True)

    target = [index_ref[0, 0:1, j * TILE:(j + 1) * TILE] for j in cuts]
    source = [index_ref[0, 1:2, j * TILE:(j + 1) * TILE] for j in cuts]
    used = [q < NSRC for q in source]
    shift = (GROUPS + GROUPS // 2 - grp) * TPS

    def order(t):
        group, tile = ((t + shift) & (DST - 1)) >> 2, t & 3
        turn = ((tile & 1) << 1) + (tile >> 1)
        near = jnp.where(group == 1, TPS + 2 * turn, TPS + 1 + 2 * (turn ^ 1))
        rest = 3 * TPS + (group - 2) * TPS + tile
        return jnp.where(group == 0, turn, jnp.where((group == 1) | (group == 7), near, rest))

    key = [jnp.where(u, order(t), DST) for u, t in zip(used, target)]
    key_col = [column(t) for t in key]
    count = sum(down(k == lane) for k in key_col)
    padded = jnp.where(lane_row < DST, (count + 1) & ~1, 0)
    padded_col = column(padded)
    begin = down(sub < lane, padded_col)
    begin_col = column(begin)
    place_col, code_col = [], []
    for j in cuts:
        rank = down((key_col[j] == key[j]) & (sub < lane))
        for i in range(j):
            rank = rank + down(key_col[i] == key[j])
        place = down(sub < key[j], padded_col) + rank
        place_col.append(column(jnp.where(used[j], place, 8 * TILE)))
        code_col.append(((j * TILE + sub) * NSRC + column(source[j])) * 2)
    for r in range(4):
        spot = lane + r * TILE
        code = jnp.full((TILE, TILE), -1, jnp.int32)
        for j in cuts:
            code = jnp.where(place_col[j] == spot, code_col[j], code)
        code = jnp.max(code, axis=0, keepdims=True)
        first = down((begin_col == spot) & (padded_col > 0))
        tblv_ref[r:r + 1, :] = jnp.where(code < 0, SLOTS * NSRC * 2, code) + first
    tblv_ref[4:5, :] = jnp.where(padded > 0, ((begin + padded) >> 1) - 1, PAIRS)
    tbl_copy = pltpu.make_async_copy(tblv_ref, tbl_ref, tbl_sem)
    tbl_copy.start()
    a_ref[SLOTS] = jnp.zeros((TILE, TILE), jnp.bfloat16)
    sum_ref[PAIRS] = jnp.zeros((TILE, TILE), jnp.float32)

    def products(segment, total):
        for pair in range(SEGMENTS[segment], SEGMENTS[segment + 1]):
            row, spot = pair // (TILE // 2), pair % (TILE // 2) * 2
            one, two = tbl_ref[row, spot], tbl_ref[row, spot + 1]
            left = jnp.concatenate([a_ref[one >> 7], a_ref[two >> 7]], axis=1)
            right = jnp.concatenate(
                [s_ref[(one >> 1) & (NSRC - 1)], s_ref[(two >> 1) & (NSRC - 1)]], axis=0)
            value = jnp.dot(left, right, preferred_element_type=jnp.float32)
            keep = (1 - (one & 1)).astype(jnp.float32)
            total = value + total * keep
            sum_ref[pair] = total
        return total

    def summed(away, part, j):
        group, turn = (away + GROUPS // 2) % GROUPS, j * PART + part
        if group == 0:
            spot = turn
        elif group == 1:
            spot = TPS + 2 * turn
        elif group == 7:
            spot = TPS + 1 + 2 * (turn ^ 1)
        else:
            spot = 3 * TPS + (group - 2) * TPS + part * PART + j
        return sum_ref[tbl_ref[4, spot]]

    def ring(m, way, j):
        reach = 4 - (m + 1) // 2
        value = summed(reach if way == 0 else GROUPS - reach, (m % 2) ^ way, j)
        for n in {3: (1,), 4: (0, 2), 5: (3,), 6: (4,)}.get(m, ()):
            wait_in(ring_in.at[way, n, j], ring_r.at[way, n, j])
            value = value + ring_in[way, n, j].astype(jnp.float32)
        ring_out[way, m, j] = value.astype(jnp.bfloat16)
        send(ring_out.at[way, m, j], ring_in.at[way, m, j],
             ring_s.at[way, m, j], ring_r.at[way, m, j], to_z2[way] if m == 0 else to_z[way])

    expected = []

    def hand(yy, i, first, count):
        number = len(expected)
        ref = tiles(yy, hs[i], c, first, count)
        send(ref, ref, sib_s.at[number], sib_r.at[number], to_sib)
        expected.append(tiles(yy, hs[i], 1 - c, first, count))

    def wait_tiles(yy, i, first, count, rsem):
        ref = tiles(yy, hs[i], c, first, count)
        wait_in(ref, rsem)
        return ref

    def over(i, turn):
        k = i ^ turn
        for v in range(2):
            send(t_ref.at[near[i], k], s_ref.at[at(near[i], h, c) * TPS + PART + k],
                 xb_s.at[2 - i, v, turn], xb_r.at[2 - i, v, turn], to_x[v])

    near = (yd, yu)
    for i in range(2):
        tile = t_ref.at[near[i], i]
        wait_in(tile, t_r.at[i, i])
        send(tile, tile, tr_s.at[i], tr_r.at[i], to_y[i])
        over(i, 0)

    def pass_on(j, i, v):
        ref = tiles(y, hs[i], c, j, 1)
        send(ref, ref, ya_s.at[v, i, j], ya_r.at[v, i, j], to_y[v])

    for i in range(2):
        wait_tiles(y, i, 0, 1, xa_r.at[0, i])
        pass_on(0, i, i)
    for i in range(2):
        wait_in(t_ref.at[near[i], 1 - i], t_r.at[i, 1 - i])
        over(i, 1)
    for i in range(2):
        wait_tiles(y, i, 1, 1, xa_r.at[1, i])
        pass_on(1, i, i)
    for j in range(PART):
        for i in range(2):
            pass_on(j, i, 1 - i)
    for i in range(2):
        hand(y, i, 0, PART)
    for i in range(2):
        wait_tiles(y, i, PART, PART, xb_r.at[0, i, 0])
        hand(y, i, PART, PART)
    for i in range(2):
        wait_in(t_ref.at[yo, i], tr_r.at[i])
        for v in range(2):
            send(t_ref.at[yo, i], s_ref.at[at(yo, h, c) * TPS + PART + i],
                 xc_s.at[i, v], xc_r.at[i, v], to_x[v])
    for j in range(PART):
        for i in range(2):
            ref = wait_tiles(near[i], i, j, 1, ya_r.at[i, i, j])
            send(ref, ref, yr_s.at[i, j], yr_r.at[i, j], to_y[i])
    for i in range(2):
        hand(near[i], i, 0, PART)
    for i in range(2):
        for v in range(2):
            for turn in range(2):
                wait_tiles(near[i], v, PART + (i ^ turn), 1, xb_r.at[2 - i, v, turn])
            hand(near[i], v, PART, PART)
    for i in range(2):
        for j in range(PART):
            wait_tiles(near[i], 1 - i, j, 1, ya_r.at[i, 1 - i, j])
        hand(near[i], 1 - i, 0, PART)
    for j in range(PART):
        for i in range(2):
            wait_tiles(yo, i, PART + j, 1, xc_r.at[j, i])
            hand(yo, i, PART + j, 1)
        for i in range(2):
            wait_tiles(yo, i, j, 1, yr_r.at[i, j])
            hand(yo, i, j, 1)
    tbl_copy.wait()
    for copy in adj_copies:
        copy.wait()
    for number, ref in enumerate(expected):
        wait_in(ref, sib_r.at[number])

    total = jnp.zeros((TILE, TILE), jnp.float32)
    early = ((0, 0, 0), (0, 1, 0), (0, 0, 1), (0, 1, 1), (1, 1, 0), (1, 0, 0))
    for segment, piece in enumerate(early):
        total = products(segment, total)
        ring(*piece)
    products(len(early), total)
    for m, j in ((2, 0), (1, 1), (2, 1)):
        for way in range(2):
            ring(m, way, j)
    for m, j in ((3, 0), (4, 0), (3, 1), (4, 1), (5, 0), (6, 0), (5, 1), (6, 1)):
        for way in range(2):
            ring(m, way, j)
    for j in range(PART):
        for m, way in ((5, 0), (5, 1), (6, 0), (6, 1)):
            wait_in(ring_in.at[way, m, j], ring_r.at[way, m, j])
        for part in range(2):
            value = summed(0, part, j) + ring_in[part, 6, j].astype(jnp.float32)
            value = value + ring_in[1 - part, 5, j].astype(jnp.float32)
            cut = pl.ds((part * PART + j) * TILE, TILE)
            out_ref[0, cut, :] = (value * inv_ref[cut, :]).astype(jnp.bfloat16)
    settle()


def shards(embed_codes, embed_exps, degrees, adjacency, block_index):
    width = embed_codes.shape[2]
    dma = pltpu.SemaphoreType.DMA
    vmem = pl.BlockSpec(memory_space=pltpu.VMEM)
    sems = []
    for shape in ((2, 2), (3, 2, 2), (2, 2), (2, 2, 2), (2, 2), (2, 2), (2,), (20,), (2, 7, PART)):
        sems += [dma(shape), dma(shape)]
    return pl.pallas_call(
        kernel,
        out_shape=jax.ShapeDtypeStruct(embed_codes.shape, jnp.bfloat16),
        in_specs=[pl.BlockSpec(memory_space=pltpu.HBM)] * 5,
        out_specs=vmem,
        scratch_shapes=[
            pltpu.VMEM((SLOTS + 1, TILE, TILE), jnp.bfloat16),
            pltpu.VMEM((NSRC, TILE, width), jnp.bfloat16),
            pltpu.VMEM((NY, TPS // 2, TILE, width), jnp.bfloat16),
            pltpu.VMEM((TPS // 2, TILE, width), jnp.bfloat16),
            pltpu.VMEM((PAIRS + 1, TILE, width), jnp.float32),
            pltpu.VMEM((ROWS, width), jnp.float32),
            pltpu.VMEM((8, TILE), jnp.int32),
            pltpu.SMEM((8, TILE), jnp.int32),
            pltpu.VMEM(embed_codes.shape, embed_codes.dtype),
            pltpu.SMEM(embed_exps.shape, embed_exps.dtype),
            pltpu.VMEM(degrees.shape, degrees.dtype),
            pltpu.VMEM(block_index.shape, block_index.dtype),
            pltpu.VMEM((2, 7, PART, TILE, width), jnp.bfloat16),
            pltpu.VMEM((2, 7, PART, TILE, width), jnp.bfloat16),
            dma((4,)), dma((ADJ_PIECES,)), dma(()),
            *sems,
        ],
        compiler_params=pltpu.CompilerParams(
            collective_id=0, has_side_effects=True, vmem_limit_bytes=67_043_328
        ),
    )(embed_codes, embed_exps, degrees, adjacency.reshape(adjacency.shape[1:]), block_index)


def solution(mesh):
    placed = (
        P("side", ("grp", "blk"), None),
        P("side", ("grp", "blk")),
        P("side", ("grp", "blk")),
        P("side", ("grp", "blk"), None, None),
        P("side", None, ("grp", "blk")),
    )
    return jax.shard_map(
        shards,
        mesh=mesh,
        in_specs=placed,
        out_specs=P("side", ("grp", "blk"), None),
        check_vma=False,
    )
```
